32 devices in a mesh: section: 2 (over x), dp: 16 (over z, y, core).
Axes of the slice: x: 2, y: 2, z: 4, core: 2. Of those that a mesh axis runs over, the one named last changes fastest.
Arguments:
- block_input: float32 [2048, 1024], P('dp'), may hold values from -6 to 6
- cotangent: float32 [2048, 1024], P('dp'), may hold values from -6 to 6
- marks: int32 [2048], P('dp'), may hold values 0 or 1
- w_in: bfloat16 [2, 1024, 4096], P('section', 'dp'), may hold values from -0.1875 to 0.1875
- w_out: bfloat16 [2, 1024, 1024], P('section', 'dp'), may hold values from -0.1875 to 0.1875
- w_up: bfloat16 [2, 1024, 5632], P('section', 'dp'), may hold values from -0.1875 to 0.1875
- w_down: bfloat16 [2, 1024, 2816], P('section', 'dp'), may hold values from -0.109375 to 0.109375
- gate_weights: bfloat16 [2, 1024, 16], P('section'), may hold values from -0.1875 to 0.1875
- norm_gains: float32 [2, 2, 1024], P('section'), may hold values from 0.5 to 1.5
- conv_weights: float32 [2, 4, 3072], P('section'), may hold values from -3 to 3
- decay_log: float32 [2, 8], P('section'), may hold values from -4 to 1
- decay_bias: float32 [2, 8], P('section'), may hold values from -4 to 0
- out_gain: float32 [2, 128], P('section'), may hold values from 0.5 to 1.5
Outputs:
- layer_outputs: float32 [2, 2048, 1024], P('section', 'dp')
- input_grads: float32 [2, 2048, 1024], P('section', 'dp')
- grad_w_in: float32 [2, 1024, 4096], P('section', 'dp')
- grad_w_out: float32 [2, 1024, 1024], P('section', 'dp')
- grad_w_up: float32 [2, 1024, 5632], P('section', 'dp')
- grad_w_down: float32 [2, 1024, 2816], P('section', 'dp')
- grad_gate_weights: float32 [2, 1024, 16], P('section')
- grad_norm_gains: float32 [2, 2, 1024], P('section')
- grad_conv_weights: float32 [2, 4, 3072], P('section')
- grad_decay_log: float32 [2, 8], P('section')
- grad_decay_bias: float32 [2, 8], P('section')
- grad_out_gain: float32 [2, 128], P('section')
The draws below stay inside these ranges and needn't reach their ends.
Inputs may be any that keep to these rules, and one draw needn't show every extreme that they name: A 1 marks the first token of a sequence; the first of every 128 rows begins a sequence whatever its mark.
All inputs are finite; a program needn't handle non-finite values. No bound on the sum of `marks` on one device may be relied on, other than what follows from the above.
Results may differ from the reference program's by a relative error of at most 0.01575.
Values may be sent and summed in bfloat16 or wider, within the bound.
A program may use at most 256 MiB of HBM per device.

```python
import jax
import jax.numpy as jnp
from jax import lax

D = 1024
FF = 2816
HEADS = 8
HEAD_DIM = 128
CONV = 4
GROUP = 64
TOK_DEV = 128
TOKENS = 2048


def touch_ends(values, own_key, smallest, high):
    place = [jax.random.randint(jax.random.fold_in(own_key, axis), (), 0, length) for axis, length in enumerate(values.shape)]
    longest = values.shape.index(max(values.shape))
    beside = place[:longest] + [(place[longest] + 1) % values.shape[longest]] + place[longest + 1:]
    return values.at[tuple(place)].set(smallest).at[tuple(beside)].set(high)


def spiked(values, key, source, target, blocks, factor):
    def block_of(axis_at):
        return (jnp.arange(values.shape[axis_at]) // (values.shape[axis_at] // blocks)).reshape((-1,) + (1,) * (values.ndim - 1 - axis_at))

    near = jax.random.permutation(key, blocks)[block_of(target)]
    second = (block_of(target) + blocks // 2) % blocks
    return jnp.where((block_of(source) == near) | (block_of(source) == second), factor * values, values)


def shard_levels(own_key, shape, split, least, largest):
    loudness, own = 1.0, jax.random.fold_in(own_key, 6)
    for dim, parts in split:
        heights = jnp.exp(jax.random.uniform(jax.random.fold_in(own, dim), (parts,), jnp.float32, least / len(split), largest / len(split)))
        loudness = loudness * jnp.repeat(heights, shape[dim] // parts).reshape([-1 if axis == dim else 1 for axis in range(len(shape))])
    return loudness


def bell_draw(own_key, extent, scale, limit, shards=(), kind=jnp.bfloat16):
    drawn = jax.random.normal(own_key, extent, jnp.float32) * scale
    if len(shards) > 0:
        drawn = shard_levels(own_key, extent, shards, -0.22, 0.18) * drawn
    return jnp.clip(drawn, min=-limit, max=limit).astype(kind)


def noise_with(rng, extent, scale, most, cuts, heavy, held_as=jnp.bfloat16):
    drawn = scale * jax.random.normal(rng, extent, jnp.float32)
    if cuts:
        drawn = drawn * shard_levels(rng, extent, cuts, -0.22, 0.18)
    return jnp.clip(spiked(drawn, jax.random.fold_in(rng, 3), *heavy), -most, most).astype(held_as)


def setup_inputs(seed: int = 0) -> dict:
    key_list = jax.random.split(jax.random.key(seed), 14)
    block_input = noise_with(key_list[0], (TOKENS, D), 1.0, 6.0, ((0, 16),), (0, 1, 16, 2.0), jnp.float32)
    cotangent = noise_with(key_list[1], (TOKENS, D), 1.0, 6.0, ((0, 16),), (0, 1, 16, 2.0), jnp.float32)
    marks = touch_ends((jax.random.randint(key_list[2], (TOKENS,), 0, 48) < 1).astype(jnp.int32), jax.random.fold_in(key_list[2], 1), 0, 1)
    w_in = bell_draw(key_list[3], (2, D, 4 * D), D ** -0.5, 0.1875, ((0, 2), (1, 16)))
    w_out = bell_draw(key_list[4], (2, D, D), D ** -0.5, 0.1875, ((0, 2), (1, 16)))
    w_up = bell_draw(key_list[5], (2, D, 2 * FF), D ** -0.5, 0.1875, ((0, 2), (1, 16)))
    w_down = bell_draw(key_list[6], (2, D, FF), FF ** -0.5, 0.109375, ((0, 2), (1, 16)))
    gate_weights = bell_draw(key_list[7], (2, D, 2 * HEADS), D ** -0.5, 0.1875, ((0, 2),))
    norm_gains = jnp.clip(1.0 + 0.1 * jax.random.normal(key_list[8], (2, 2, D), jnp.float32), 0.5, 1.5)
    conv_weights = bell_draw(key_list[9], (2, CONV, 3 * D), CONV ** -0.5, 3.0, ((0, 2),), jnp.float32)
    decay_log = jnp.clip(-4.0 + 5.0 * jax.random.uniform(key_list[10], (2, HEADS), jnp.float32) ** shard_levels(key_list[10], (2, HEADS), ((0, 2),), -0.2, 0.2), -4.0, 1.0)
    decay_bias = jnp.clip(-4.0 + 4.0 * jax.random.uniform(key_list[11], (2, HEADS), jnp.float32) ** shard_levels(key_list[11], (2, HEADS), ((0, 2),), -0.2, 0.2), -4.0, 0.0)
    out_gain = jnp.clip(1.0 + 0.1 * jax.random.normal(key_list[12], (2, HEAD_DIM), jnp.float32), 0.5, 1.5)
    return dict(block_input=block_input, cotangent=cotangent, marks=marks, w_in=w_in, w_out=w_out, w_up=w_up, w_down=w_down, gate_weights=gate_weights, norm_gains=norm_gains, conv_weights=conv_weights, decay_log=decay_log, decay_bias=decay_bias, out_gain=out_gain)


epsilon = 1e-06
highest = lax.Precision.HIGHEST

def dot_rows(left, right):
    return lax.dot_general(left.astype(jnp.float32), right.astype(jnp.float32), (((1,), (1,)), ((), ())), preferred_element_type=jnp.float32)

def dot_cols(left, right):
    return lax.dot_general(left.astype(jnp.float32), right.astype(jnp.float32), (((0,), (0,)), ((), ())), preferred_element_type=jnp.float32)

def rms_scale(values, gain):
    return values * lax.rsqrt(lax.optimization_barrier(jnp.mean(values * values, axis=-1, keepdims=True)) + epsilon) * gain

def segment_ids(marks_block):
    position = jnp.arange(marks_block.shape[0])
    starts = jnp.logical_or(marks_block > 0, position == 0).astype(jnp.int32)
    return jnp.cumsum(starts).astype(jnp.int32)

def short_conv(columns, kernel, segment):
    row_count, width = columns.shape
    total = columns * kernel[CONV - 1]
    for offset in range(1, CONV):
        shifted = jnp.concatenate([jnp.zeros((offset, width), columns.dtype), columns[:row_count - offset]], axis=0)
        same = jnp.concatenate([jnp.zeros((offset,), jnp.bool_), segment[offset:] == segment[:row_count - offset]])
        total = total + jnp.where(same[:, None], shifted, 0.0) * kernel[CONV - 1 - offset]
    return jax.nn.silu(total)

def delta_rule(queries, key_rows, value_rows, beta_rows, log_decay, segment):
    row_count = queries.shape[0]
    blocks = row_count // GROUP

    def to_blocks(array):
        shaped = array.reshape((blocks, GROUP, HEADS) + array.shape[2:])
        return jnp.moveaxis(shaped, 2, 1)
    seg_blocks = segment.reshape(blocks, GROUP)
    before = jnp.concatenate([jnp.full((1,), -1, jnp.int32), seg_blocks[:-1, GROUP - 1]]).astype(jnp.int32)
    index_a = jnp.arange(GROUP)[:, None]
    index_b = jnp.arange(GROUP)[None, :]
    lower = index_a >= index_b
    strict = index_a > index_b
    identity = jnp.eye(GROUP, dtype=jnp.float32)

    def step_block(state, inputs):
        query_b, key_b, value_b, beta_b, decay_b, seg_b, prior = inputs
        cumul = jnp.cumsum(decay_b, axis=1)
        within = jnp.logical_and(seg_b[:, None] == seg_b[None, :], lower)
        spread = cumul[:, :, None] - cumul[:, None, :]
        weights_in = jnp.where(within[None], jnp.exp(jnp.minimum(spread, 0.0)), 0.0)
        carried = jnp.where((seg_b == prior)[None, :], jnp.exp(cumul), 0.0)
        key_key = jnp.einsum('hid,hjd->hij', key_b, key_b, precision=highest)
        left_side = identity + jnp.where(strict[None], weights_in, 0.0) * key_key * beta_b[:, :, None]
        state_keys = jnp.einsum('hid,hed->hie', key_b, state, precision=highest)
        right_side = beta_b[:, :, None] * (value_b - carried[:, :, None] * state_keys)
        pseudo = lax.linalg.triangular_solve(left_side, right_side, left_side=True, lower=True, unit_diagonal=True)
        query_key = jnp.einsum('hid,hjd->hij', query_b, key_b, precision=highest)
        state_query = jnp.einsum('hid,hed->hie', query_b, state, precision=highest)
        output = carried[:, :, None] * state_query + jnp.einsum('hij,hje->hie', query_key * weights_in, pseudo, precision=highest)
        tail = weights_in[:, GROUP - 1, :]
        state = carried[:, GROUP - 1][:, None, None] * state + jnp.einsum('hje,hjd->hed', pseudo * tail[:, :, None], key_b, precision=highest)
        return (state, output)
    start_state = jnp.zeros((HEADS, HEAD_DIM, HEAD_DIM), jnp.float32)
    inputs = (to_blocks(queries), to_blocks(key_rows), to_blocks(value_rows), to_blocks(beta_rows), to_blocks(log_decay), seg_blocks, before)
    _, outputs = lax.scan(step_block, start_state, inputs)
    return jnp.moveaxis(outputs, 1, 2).reshape(row_count, HEADS, HEAD_DIM)

def mixer_core(proj, gate_pre, kernel, decay_log, decay_bias, out_gain, segment):
    row_count = proj.shape[0]
    mixed_in = short_conv(proj[:, :3 * D], kernel, segment)
    heads_shape = (row_count, HEADS, HEAD_DIM)
    query_raw = mixed_in[:, :D].reshape(heads_shape)
    key_raw = mixed_in[:, D:2 * D].reshape(heads_shape)
    value_rows = mixed_in[:, 2 * D:].reshape(heads_shape)
    queries = query_raw * lax.rsqrt(lax.optimization_barrier(jnp.sum(query_raw * query_raw, axis=-1, keepdims=True)) + epsilon) * HEAD_DIM ** (-0.5)
    key_rows = key_raw * lax.rsqrt(lax.optimization_barrier(jnp.sum(key_raw * key_raw, axis=-1, keepdims=True)) + epsilon)
    beta_rows = jax.nn.sigmoid(gate_pre[:, HEADS:])
    log_decay = -jnp.exp(decay_log) * jax.nn.softplus(gate_pre[:, :HEADS] + decay_bias)
    delta_out = delta_rule(queries, key_rows, value_rows, beta_rows, log_decay, segment)
    scaled = delta_out * lax.rsqrt(lax.optimization_barrier(jnp.mean(delta_out * delta_out, axis=-1, keepdims=True)) + epsilon) * out_gain
    gate_part = proj[:, 3 * D:].reshape(heads_shape)
    return (scaled * jax.nn.silu(gate_part)).reshape(row_count, D)

def swiglu(upgate):
    return jax.nn.silu(upgate[:, :FF]) * upgate[:, FF:]

def layer_forward(w_in, w_out, w_up, w_down, gate_weights, norm_gains, kernel, decay_log, decay_bias, out_gain, block, marks_block):
    segment = segment_ids(marks_block)
    normed_a = rms_scale(block, norm_gains[0]).astype(jnp.bfloat16)
    proj = jnp.dot(normed_a.astype(jnp.float32), w_in.astype(jnp.float32), preferred_element_type=jnp.float32)
    gate_pre = jnp.dot(normed_a.astype(jnp.float32), gate_weights.astype(jnp.float32), preferred_element_type=jnp.float32)
    mixer = mixer_core(proj, gate_pre, kernel, decay_log, decay_bias, out_gain, segment).astype(jnp.bfloat16)
    middle = block + jnp.dot(mixer.astype(jnp.float32), w_out.astype(jnp.float32), preferred_element_type=jnp.float32)
    normed_f = rms_scale(middle, norm_gains[1]).astype(jnp.bfloat16)
    upgate = jnp.dot(normed_f.astype(jnp.float32), w_up.astype(jnp.float32), preferred_element_type=jnp.float32)
    hidden = swiglu(upgate).astype(jnp.bfloat16)
    result = middle + dot_rows(hidden, w_down)
    return (result, (normed_a, proj, gate_pre, mixer, middle, normed_f, upgate, hidden))

def layer_backward(w_in, w_out, w_up, w_down, gate_weights, norm_gains, kernel, decay_log, decay_bias, out_gain, block, marks_block, saved, grad_out):
    segment = segment_ids(marks_block)
    normed_a, proj, gate_pre, mixer, middle, normed_f, upgate, hidden = saved
    g_bf = grad_out.astype(jnp.bfloat16)
    d_hidden = jnp.dot(g_bf.astype(jnp.float32), w_down.astype(jnp.float32), preferred_element_type=jnp.float32)
    _, swiglu_back = jax.vjp(swiglu, upgate)
    d_upgate = swiglu_back(d_hidden)[0].astype(jnp.bfloat16)
    d_normed_f = dot_rows(d_upgate, w_up)
    _, norm_back_f = jax.vjp(rms_scale, middle, norm_gains[1])
    d_middle, gain_f = norm_back_f(d_normed_f)
    d_middle = d_middle + grad_out
    dm_bf = d_middle.astype(jnp.bfloat16)
    d_mixer = dot_rows(dm_bf, w_out)

    def core_of(proj_in, gate_in, kernel_in, log_in, bias_in, gain_in):
        return mixer_core(proj_in, gate_in, kernel_in, log_in, bias_in, gain_in, segment)
    _, core_back = jax.vjp(core_of, proj, gate_pre, kernel, decay_log, decay_bias, out_gain)
    d_proj, d_gate_pre, d_kernel, d_log, d_bias, d_gain = core_back(d_mixer)
    d_proj = d_proj.astype(jnp.bfloat16)
    d_gate_pre = d_gate_pre.astype(jnp.bfloat16)
    d_normed_a = dot_rows(d_proj, w_in) + dot_rows(d_gate_pre, gate_weights)
    _, norm_back_a = jax.vjp(rms_scale, block, norm_gains[0])
    d_block, gain_a = norm_back_a(d_normed_a)
    d_block = d_block + d_middle
    small = (dot_cols(normed_a, d_gate_pre), jnp.stack([gain_a, gain_f]), d_kernel, d_log, d_bias, d_gain)
    factors = (normed_a, d_proj, mixer, dm_bf, normed_f, d_upgate, g_bf, hidden)
    return (d_block, small, factors)

def weight_terms(factors, start, count):
    normed_a, d_proj, mixer, dm_bf, normed_f, d_upgate, g_bf, hidden = factors

    def part(left, right):
        columns = lax.dynamic_slice_in_dim(left, start, count, 1)
        return dot_cols(columns, right)
    return jnp.concatenate([part(normed_a, d_proj), part(mixer, dm_bf), part(normed_f, d_upgate), part(g_bf, hidden)], axis=1)

def reference(block_input, cotangent, marks, w_in, w_out, w_up, w_down, gate_weights, norm_gains, conv_weights, decay_log, decay_bias, out_gain):
    blocks = TOKENS // TOK_DEV
    mark_blocks = marks.reshape(blocks, TOK_DEV)

    def params_of(layer):
        return (w_in[layer], w_out[layer], w_up[layer], w_down[layer], gate_weights[layer], norm_gains[layer], conv_weights[layer], decay_log[layer], decay_bias[layer], out_gain[layer])

    def forward_layer(layer, values):
        params = params_of(layer)
        pieces = values.reshape(blocks, TOK_DEV, D)
        outputs = lax.map(lambda item: layer_forward(*params, item[0], item[1])[0], (pieces, mark_blocks))
        return outputs.reshape(TOKENS, D)

    def backward_layer(layer, values, grads):
        params = params_of(layer)

        def step_block(carry, item):
            piece, mark_piece, grad_piece = item
            _, saved = layer_forward(*params, piece, mark_piece)
            d_block, small, factors = layer_backward(*params, piece, mark_piece, saved, grad_piece)
            big = carry[0] + weight_terms(factors, 0, D)
            rest = jax.tree.map(jnp.add, carry[1], small)
            return ((big, rest), d_block)
        start_small = (jnp.zeros((D, 2 * HEADS), jnp.float32), jnp.zeros((2, D), jnp.float32), jnp.zeros((CONV, 3 * D), jnp.float32), jnp.zeros((HEADS,), jnp.float32), jnp.zeros((HEADS,), jnp.float32), jnp.zeros((HEAD_DIM,), jnp.float32))
        start = (jnp.zeros((D, 5 * D + 3 * FF), jnp.float32), start_small)
        inputs = (values.reshape(blocks, TOK_DEV, D), mark_blocks, grads.reshape(blocks, TOK_DEV, D))
        (big, small), d_blocks = lax.scan(step_block, start, inputs)
        return (d_blocks.reshape(TOKENS, D), big, small)
    first_out = forward_layer(0, block_input)
    second_out = forward_layer(1, first_out)
    second_grad, second_big, second_small = backward_layer(1, first_out, cotangent)
    first_grad, first_big, first_small = backward_layer(0, block_input, second_grad)
    bigs = jnp.stack([first_big, second_big])
    smalls = jax.tree.map(lambda a, b: jnp.stack([a, b]), first_small, second_small)
    return (jnp.stack([first_out, second_out]), jnp.stack([first_grad, second_grad]), bigs[:, :, :4 * D], bigs[:, :, 4 * D:5 * D], bigs[:, :, 5 * D:5 * D + 2 * FF], bigs[:, :, 5 * D + 2 * FF:], smalls[0], smalls[1], smalls[2], smalls[3], smalls[4], smalls[5])
```

```python
import jax
import jax.numpy as jnp
from jax import lax
from jax.experimental import pallas as pl
from jax.sharding import PartitionSpec as P

D = 1024
FF = 2816
HEADS = 8
HEAD_DIM = 128
CONV = 4
BLOCK = 128
GROUP_HEADS = 4


epsilon = 1e-06
highest = lax.Precision.HIGHEST


def passed_along(value, axis, steps):
    count = lax.axis_size(axis)
    initial, last = (max(0, -steps), min(count, count - steps))
    return lax.ppermute(value, axis, [(source, source + steps) for source in range(initial, last)])


def dot_rows(left, right):
    return lax.dot_general(
        left, right, (((1,), (1,)), ((), ())), preferred_element_type=jnp.float32
    )


def dot_cols(left, right):
    return lax.dot_general(
        left, right, (((0,), (0,)), ((), ())), preferred_element_type=jnp.float32
    )


def rms_scale(values, gain):
    return values * lax.rsqrt(jnp.mean(values * values, axis=-1, keepdims=True) + epsilon) * gain


def segment_ids(marks_block):
    position = jnp.arange(marks_block.shape[0])
    starts = jnp.logical_or(marks_block > 0, position == 0).astype(jnp.int32)
    return jnp.cumsum(starts)


def short_conv(columns, kernel, segment):
    row_count, width = columns.shape
    total = columns * kernel[CONV - 1]
    for offset in range(1, CONV):
        shifted = jnp.concatenate(
            [jnp.zeros((offset, width), columns.dtype), columns[: row_count - offset]], axis=0
        )
        same = jnp.concatenate(
            [jnp.zeros((offset,), jnp.bool_), segment[offset:] == segment[: row_count - offset]]
        )
        total = total + jnp.where(same[:, None], shifted, 0.0) * kernel[CONV - 1 - offset]
    return jax.nn.silu(total)


def triangle(seg_col, seg_row):
    row = lax.broadcasted_iota(jnp.int32, (BLOCK, BLOCK), 0)
    col = lax.broadcasted_iota(jnp.int32, (BLOCK, BLOCK), 1)
    within = jnp.logical_and(seg_col == seg_row, row >= col)
    return row, col, within


def mm(left, right, dims):
    return lax.dot_general(
        left, right, (dims, ((), ())), precision=highest, preferred_element_type=jnp.float32
    )


NN = ((1,), (0,))
NT = ((1,), (1,))
TN = ((0,), (0,))


def delta_fwd_kernel(
    q_ref, k_ref, v_ref, beta_ref, ccol_ref, crow_ref, scol_ref, srow_ref, o_ref, t_ref, p_ref
):
    row, col, within = triangle(scol_ref[...], srow_ref[0])
    apart = jnp.bitwise_xor(row, col)
    eye = (row == col).astype(jnp.float32)
    heads = range(GROUP_HEADS)
    at = [pl.ds(h * HEAD_DIM, HEAD_DIM) for h in heads]
    weights = [
        jnp.where(within, jnp.exp(jnp.minimum(ccol_ref[h] - crow_ref[h], 0.0)), 0.0) for h in heads
    ]
    keys = [k_ref[:, at[h]] for h in heads]
    below = [
        jnp.where(row > col, weights[h], 0.0) * mm(keys[h], keys[h], NT) * beta_ref[h]
        for h in heads
    ]
    inverse = [eye - jnp.where(apart == 1, below[h], 0.0) for h in heads]
    size = 2
    while size < BLOCK:
        level = jnp.logical_and(apart >= size, apart < 2 * size)
        inner = [mm(jnp.where(level, below[h], 0.0), inverse[h], NN) for h in heads]
        inverse = [inverse[h] - mm(inverse[h], inner[h], NN) for h in heads]
        size *= 2
    pseudo = [mm(inverse[h], beta_ref[h] * v_ref[:, at[h]], NN) for h in heads]
    for h in heads:
        score = mm(q_ref[:, at[h]], keys[h], NT) * weights[h]
        o_ref[:, at[h]] = mm(score, pseudo[h], NN)
        t_ref[:, at[h]] = inverse[h]
        p_ref[:, at[h]] = pseudo[h]


def delta_bwd_kernel(
    q_ref,
    k_ref,
    v_ref,
    beta_ref,
    ccol_ref,
    crow_ref,
    scol_ref,
    srow_ref,
    t_ref,
    p_ref,
    do_ref,
    dq_ref,
    dk_ref,
    dv_ref,
    dbeta_ref,
    dccol_ref,
    dcrow_ref,
):
    row, col, within = triangle(scol_ref[...], srow_ref[0])
    strict = row > col
    for h in range(GROUP_HEADS):
        at = pl.ds(h * HEAD_DIM, HEAD_DIM)
        weights = jnp.where(within, jnp.exp(jnp.minimum(ccol_ref[h] - crow_ref[h], 0.0)), 0.0)
        query, key, value, beta = q_ref[:, at], k_ref[:, at], v_ref[:, at], beta_ref[h]
        pseudo, d_out = p_ref[:, at], do_ref[:, at]
        key_key = mm(key, key, NT)
        query_key = mm(query, key, NT)
        d_score = mm(d_out, pseudo, NT)
        d_pseudo = mm(query_key * weights, d_out, TN)
        d_right = mm(t_ref[:, at], d_pseudo, TN)
        d_left = jnp.where(strict, -mm(d_right, pseudo, NT), 0.0)
        dv_ref[:, at] = beta * d_right
        left_key = d_left * weights
        dbeta_ref[h] = jnp.sum(d_right * value, axis=1, keepdims=True) + jnp.sum(
            left_key * key_key, axis=1, keepdims=True
        )
        d_query_key = d_score * weights
        d_key_key = left_key * beta
        dq_ref[:, at] = mm(d_query_key, key, NN)
        dk_ref[:, at] = (
            mm(d_query_key, query, TN) + mm(d_key_key, key, NN) + mm(d_key_key, key, TN)
        )
        d_spread = d_query_key * query_key + d_key_key * key_key
        dccol_ref[h] = jnp.sum(d_spread, axis=1, keepdims=True)
        dcrow_ref[h] = jnp.sum(d_spread, axis=0, keepdims=True)


def delta_call(kernel, ins, kinds, outs, flops):
    rows = ins[0].shape[0]
    wide = pl.BlockSpec((BLOCK, GROUP_HEADS * HEAD_DIM), lambda b, g: (b, g))
    column = pl.BlockSpec((GROUP_HEADS, BLOCK, 1), lambda b, g: (g, b, 0))
    flat = pl.BlockSpec((GROUP_HEADS, 1, BLOCK), lambda b, g: (g, 0, b))
    seg_column = pl.BlockSpec((BLOCK, 1), lambda b, g: (b, 0))
    seg_flat = pl.BlockSpec((1, 1, BLOCK), lambda b, g: (0, 0, b))
    specs = {"w": wide, "c": column, "r": flat, "s": seg_column, "t": seg_flat}
    shapes = {"w": (rows, HEADS * HEAD_DIM), "c": (HEADS, rows, 1), "r": (HEADS, 1, rows)}
    return pl.pallas_call(
        kernel,
        grid=(rows // BLOCK, HEADS // GROUP_HEADS),
        in_specs=[specs[kind] for kind in kinds],
        out_specs=[specs[kind] for kind in outs],
        out_shape=[jax.ShapeDtypeStruct(shapes[kind], jnp.float32) for kind in outs],
        cost_estimate=pl.CostEstimate(
            flops=flops * rows * BLOCK * D, bytes_accessed=40 * rows * D, transcendentals=rows * D
        ),
    )(*ins)


@jax.custom_vjp
def delta_core(queries, keys, values, beta, cumul, segment):
    return delta_core_fwd(queries, keys, values, beta, cumul, segment)[0]


def delta_core_fwd(queries, keys, values, beta, cumul, segment):
    ins = (
        queries,
        keys,
        values,
        beta.T[:, :, None],
        cumul.T[:, :, None],
        cumul.T[:, None, :],
        segment[:, None],
        segment[None, None, :],
    )
    out, inverse, pseudo = delta_call(delta_fwd_kernel, ins, "wwwccrst", "www", 200)
    return out, (ins, inverse, pseudo)


def delta_core_bwd(saved, d_out):
    ins, inverse, pseudo = saved
    d_q, d_k, d_v, d_beta, d_col, d_row = delta_call(
        delta_bwd_kernel, ins + (inverse, pseudo, d_out), "wwwccrstwww", "wwwccr", 120
    )
    d_cumul = (d_col[:, :, 0] - d_row[:, 0, :]).T
    return d_q, d_k, d_v, d_beta[:, :, 0].T, d_cumul, None


delta_core.defvjp(delta_core_fwd, delta_core_bwd)


def delta_rule(queries, key_rows, value_rows, beta_rows, log_decay, segment):
    rows = queries.shape[0]
    cumul = jnp.cumsum(log_decay.reshape(rows // BLOCK, BLOCK, HEADS), axis=1).reshape(rows, HEADS)

    def wide(array):
        return array.reshape(rows, HEADS * HEAD_DIM)

    out = delta_core(
        wide(queries), wide(key_rows), wide(value_rows), beta_rows, cumul, segment
    )
    return out.reshape(rows, HEADS, HEAD_DIM)


def mixer_core(proj, gate_pre, kernel, decay_log, decay_bias, out_gain, segment):
    row_count = proj.shape[0]
    mixed_in = short_conv(proj[:, : 3 * D], kernel, segment)
    heads_shape = (row_count, HEADS, HEAD_DIM)
    query_raw = mixed_in[:, :D].reshape(heads_shape)
    key_raw = mixed_in[:, D : 2 * D].reshape(heads_shape)
    value_rows = mixed_in[:, 2 * D :].reshape(heads_shape)
    queries = (
        query_raw
        * lax.rsqrt(jnp.sum(query_raw * query_raw, axis=-1, keepdims=True) + epsilon)
        * HEAD_DIM ** (-0.5)
    )
    key_rows = key_raw * lax.rsqrt(jnp.sum(key_raw * key_raw, axis=-1, keepdims=True) + epsilon)
    beta_rows = jax.nn.sigmoid(gate_pre[:, HEADS:])
    log_decay = -jnp.exp(decay_log) * jax.nn.softplus(gate_pre[:, :HEADS] + decay_bias)
    delta_out = delta_rule(queries, key_rows, value_rows, beta_rows, log_decay, segment)
    scaled = (
        delta_out
        * lax.rsqrt(jnp.mean(delta_out * delta_out, axis=-1, keepdims=True) + epsilon)
        * out_gain
    )
    gate_part = proj[:, 3 * D :].reshape(heads_shape)
    return (scaled * jax.nn.silu(gate_part)).reshape(row_count, D)


def swiglu(upgate):
    return jax.nn.silu(upgate[:, :FF]) * upgate[:, FF:]


def layer_forward(weights, small_params, block, segment):
    w_in, w_out, w_up, w_down = weights
    gate_weights, norm_gains, kernel, decay_log, decay_bias, out_gain = small_params
    normed_a = rms_scale(block, norm_gains[0]).astype(jnp.bfloat16)
    proj = jnp.dot(normed_a, w_in, preferred_element_type=jnp.float32)
    gate_pre = jnp.dot(normed_a, gate_weights, preferred_element_type=jnp.float32)

    def core_of(proj_in, gate_in, kernel_in, log_in, bias_in, gain_in):
        return mixer_core(proj_in, gate_in, kernel_in, log_in, bias_in, gain_in, segment)

    mixer, core_back = jax.vjp(
        core_of, proj, gate_pre, kernel, decay_log, decay_bias, out_gain
    )
    mixer = mixer.astype(jnp.bfloat16)
    middle = block + jnp.dot(mixer, w_out, preferred_element_type=jnp.float32)
    normed_f = rms_scale(middle, norm_gains[1]).astype(jnp.bfloat16)
    upgate = jnp.dot(normed_f, w_up, preferred_element_type=jnp.float32)
    hidden = swiglu(upgate).astype(jnp.bfloat16)
    result = middle + dot_rows(hidden, w_down)
    return (result, (normed_a, core_back, mixer, middle, normed_f, upgate, hidden))


def summed_rows(left, right):
    part = dot_cols(left, right).astype(jnp.bfloat16)
    return lax.psum_scatter(part, "dp", scatter_dimension=0, tiled=True).astype(jnp.float32)


def layer_backward(weights, small_params, block, saved, grad_out, sums):
    w_in, w_out, w_up, w_down = weights
    gate_weights, norm_gains = small_params[:2]
    normed_a, core_back, mixer, middle, normed_f, upgate, hidden = saved
    g_bf = grad_out.astype(jnp.bfloat16)
    d_hidden = jnp.dot(g_bf, w_down, preferred_element_type=jnp.float32)
    _, swiglu_back = jax.vjp(swiglu, upgate)
    d_upgate = swiglu_back(d_hidden)[0].astype(jnp.bfloat16)
    d_normed_f = dot_rows(d_upgate, w_up)
    _, norm_back_f = jax.vjp(rms_scale, middle, norm_gains[1])
    d_middle, gain_f = norm_back_f(d_normed_f)
    d_middle = d_middle + grad_out
    dm_bf = d_middle.astype(jnp.bfloat16)
    d_mixer = dot_rows(dm_bf, w_out)
    d_proj, d_gate_pre, d_kernel, d_log, d_bias, d_gain = core_back(d_mixer)
    d_proj = d_proj.astype(jnp.bfloat16)
    d_gate_pre = d_gate_pre.astype(jnp.bfloat16)
    d_normed_a = dot_rows(d_proj, w_in) + dot_rows(d_gate_pre, gate_weights)
    _, norm_back_a = jax.vjp(rms_scale, block, norm_gains[0])
    d_block, gain_a = norm_back_a(d_normed_a)
    d_block = d_block + d_middle
    if not sums:
        return d_block
    big = (
        summed_rows(normed_a, d_proj),
        summed_rows(mixer, dm_bf),
        summed_rows(normed_f, d_upgate),
        summed_rows(g_bf, hidden),
    )
    small = (
        dot_cols(normed_a, d_gate_pre),
        jnp.stack([gain_a, gain_f]),
        d_kernel,
        d_log,
        d_bias,
        d_gain,
    )
    return (d_block, big, small)


def summed_small(parts):
    flat = jnp.concatenate([part.reshape(-1) for part in parts])
    flat = lax.psum(flat, "dp")
    outs, start = [], 0
    for part in parts:
        outs.append(flat[start : start + part.size].reshape(part.shape))
        start += part.size
    return outs


def local(
    block_input,
    cotangent,
    marks,
    w_in,
    w_out,
    w_up,
    w_down,
    gate_weights,
    norm_gains,
    conv_weights,
    decay_log,
    decay_bias,
    out_gain,
):
    first_section = lax.axis_index("section") == 0
    small_params = (
        gate_weights[0],
        norm_gains[0],
        conv_weights[0],
        decay_log[0],
        decay_bias[0],
        out_gain[0],
    )
    weights = tuple(
        lax.all_gather(weight[0], "dp", axis=0, tiled=True) for weight in (w_in, w_out, w_up, w_down)
    )
    segment = segment_ids(marks)
    early_out, _ = layer_forward(weights, small_params, block_input, segment)
    arrived = passed_along(early_out.astype(jnp.bfloat16), "section", 1).astype(jnp.float32)
    source = jnp.where(first_section, block_input, arrived)
    layer_out, saved = layer_forward(weights, small_params, source, segment)
    late_grad = layer_backward(weights, small_params, source, saved, cotangent, False)
    returned = passed_along(late_grad.astype(jnp.bfloat16), "section", -1).astype(jnp.float32)
    grad_out = jnp.where(first_section, returned, cotangent)
    input_grad, big, small = layer_backward(weights, small_params, source, saved, grad_out, True)
    return tuple(part[None] for part in (layer_out, input_grad, *big, *summed_small(small)))


def solution(mesh):
    return jax.shard_map(
        local,
        mesh=mesh,
        in_specs=(
            P("dp", None),
            P("dp", None),
            P("dp"),
            P("section", "dp", None),
            P("section", "dp", None),
            P("section", "dp", None),
            P("section", "dp", None),
            P("section", None, None),
            P("section", None, None),
            P("section", None, None),
            P("section", None),
            P("section", None),
            P("section", None),
        ),
        out_specs=(
            P("section", "dp", None),
            P("section", "dp", None),
            P("section", "dp", None),
            P("section", "dp", None),
            P("section", "dp", None),
            P("section", "dp", None),
            P("section", None, None),
            P("section", None, None),
            P("section", None, None),
            P("section", None),
            P("section", None),
            P("section", None),
        ),
        check_vma=False,
    )
```

```python
import jax
import jax.numpy as jnp
from jax import lax
from jax.experimental import pallas as pl
from jax.sharding import PartitionSpec as P

D = 1024
FF = 2816
HEADS = 8
HEAD_DIM = 128
CONV = 4
BLOCK = 128
GROUP_HEADS = 4


epsilon = 1e-06
highest = lax.Precision.HIGHEST


def passed_along(value, axis, steps):
    count = lax.axis_size(axis)
    initial, last = (max(0, -steps), min(count, count - steps))
    return lax.ppermute(value, axis, [(source, source + steps) for source in range(initial, last)])


def dot_rows(left, right):
    return lax.dot_general(
        left, right, (((1,), (1,)), ((), ())), preferred_element_type=jnp.float32
    )


def dot_cols(left, right):
    return lax.dot_general(
        left, right, (((0,), (0,)), ((), ())), preferred_element_type=jnp.float32
    )


def rms_scale(values, gain):
    return values * lax.rsqrt(jnp.mean(values * values, axis=-1, keepdims=True) + epsilon) * gain


def segment_ids(marks_block):
    position = jnp.arange(marks_block.shape[0])
    starts = jnp.logical_or(marks_block > 0, position == 0).astype(jnp.int32)
    return jnp.cumsum(starts)


def short_conv(columns, kernel, segment):
    row_count, width = columns.shape
    total = columns * kernel[CONV - 1]
    for offset in range(1, CONV):
        shifted = jnp.concatenate(
            [jnp.zeros((offset, width), columns.dtype), columns[: row_count - offset]], axis=0
        )
        same = jnp.concatenate(
            [jnp.zeros((offset,), jnp.bool_), segment[offset:] == segment[: row_count - offset]]
        )
        total = total + jnp.where(same[:, None], shifted, 0.0) * kernel[CONV - 1 - offset]
    return jax.nn.silu(total)


def triangle(seg_col, seg_row):
    row = lax.broadcasted_iota(jnp.int32, (BLOCK, BLOCK), 0)
    col = lax.broadcasted_iota(jnp.int32, (BLOCK, BLOCK), 1)
    within = jnp.logical_and(seg_col == seg_row, row >= col)
    return row, col, within


def mm(left, right, dims):
    return lax.dot_general(
        left, right, (dims, ((), ())), precision=highest, preferred_element_type=jnp.float32
    )


NN = ((1,), (0,))
NT = ((1,), (1,))
TN = ((0,), (0,))


def delta_fwd_kernel(
    q_ref, k_ref, v_ref, beta_ref, ccol_ref, crow_ref, scol_ref, srow_ref, o_ref, t_ref, p_ref
):
    row, col, within = triangle(scol_ref[...], srow_ref[0])
    apart = jnp.bitwise_xor(row, col)
    eye = (row == col).astype(jnp.float32)
    heads = range(GROUP_HEADS)
    at = [pl.ds(h * HEAD_DIM, HEAD_DIM) for h in heads]
    weights = [
        jnp.where(within, jnp.exp(jnp.minimum(ccol_ref[h] - crow_ref[h], 0.0)), 0.0) for h in heads
    ]
    keys = [k_ref[:, at[h]] for h in heads]
    below = [
        jnp.where(row > col, weights[h], 0.0) * mm(keys[h], keys[h], NT) * beta_ref[h]
        for h in heads
    ]
    inverse = [eye - jnp.where(apart == 1, below[h], 0.0) for h in heads]
    size = 2
    while size < BLOCK:
        level = jnp.logical_and(apart >= size, apart < 2 * size)
        inner = [mm(jnp.where(level, below[h], 0.0), inverse[h], NN) for h in heads]
        inverse = [inverse[h] - mm(inverse[h], inner[h], NN) for h in heads]
        size *= 2
    pseudo = [mm(inverse[h], beta_ref[h] * v_ref[:, at[h]], NN) for h in heads]
    for h in heads:
        score = mm(q_ref[:, at[h]], keys[h], NT) * weights[h]
        o_ref[:, at[h]] = mm(score, pseudo[h], NN)
        t_ref[:, at[h]] = inverse[h]
        p_ref[:, at[h]] = pseudo[h]


def delta_bwd_kernel(
    q_ref,
    k_ref,
    v_ref,
    beta_ref,
    ccol_ref,
    crow_ref,
    scol_ref,
    srow_ref,
    t_ref,
    p_ref,
    do_ref,
    dq_ref,
    dk_ref,
    dv_ref,
    dbeta_ref,
    dccol_ref,
    dcrow_ref,
):
    row, col, within = triangle(scol_ref[...], srow_ref[0])
    strict = row > col
    for h in range(GROUP_HEADS):
        at = pl.ds(h * HEAD_DIM, HEAD_DIM)
        weights = jnp.where(within, jnp.exp(jnp.minimum(ccol_ref[h] - crow_ref[h], 0.0)), 0.0)
        query, key, value, beta = q_ref[:, at], k_ref[:, at], v_ref[:, at], beta_ref[h]
        pseudo, d_out = p_ref[:, at], do_ref[:, at]
        key_key = mm(key, key, NT)
        query_key = mm(query, key, NT)
        d_score = mm(d_out, pseudo, NT)
        d_pseudo = mm(query_key * weights, d_out, TN)
        d_right = mm(t_ref[:, at], d_pseudo, TN)
        d_left = jnp.where(strict, -mm(d_right, pseudo, NT), 0.0)
        dv_ref[:, at] = beta * d_right
        left_key = d_left * weights
        dbeta_ref[h] = jnp.sum(d_right * value, axis=1, keepdims=True) + jnp.sum(
            left_key * key_key, axis=1, keepdims=True
        )
        d_query_key = d_score * weights
        d_key_key = left_key * beta
        dq_ref[:, at] = mm(d_query_key, key, NN)
        dk_ref[:, at] = (
            mm(d_query_key, query, TN) + mm(d_key_key, key, NN) + mm(d_key_key, key, TN)
        )
        d_spread = d_query_key * query_key + d_key_key * key_key
        dccol_ref[h] = jnp.sum(d_spread, axis=1, keepdims=True)
        dcrow_ref[h] = jnp.sum(d_spread, axis=0, keepdims=True)


def delta_call(kernel, ins, kinds, outs, flops):
    rows = ins[0].shape[0]
    wide = pl.BlockSpec((BLOCK, GROUP_HEADS * HEAD_DIM), lambda b, g: (b, g))
    column = pl.BlockSpec((GROUP_HEADS, BLOCK, 1), lambda b, g: (g, b, 0))
    flat = pl.BlockSpec((GROUP_HEADS, 1, BLOCK), lambda b, g: (g, 0, b))
    seg_column = pl.BlockSpec((BLOCK, 1), lambda b, g: (b, 0))
    seg_flat = pl.BlockSpec((1, 1, BLOCK), lambda b, g: (0, 0, b))
    specs = {"w": wide, "c": column, "r": flat, "s": seg_column, "t": seg_flat}
    shapes = {"w": (rows, HEADS * HEAD_DIM), "c": (HEADS, rows, 1), "r": (HEADS, 1, rows)}
    return pl.pallas_call(
        kernel,
        grid=(rows // BLOCK, HEADS // GROUP_HEADS),
        in_specs=[specs[kind] for kind in kinds],
        out_specs=[specs[kind] for kind in outs],
        out_shape=[jax.ShapeDtypeStruct(shapes[kind], jnp.float32) for kind in outs],
        cost_estimate=pl.CostEstimate(
            flops=flops * rows * BLOCK * D, bytes_accessed=40 * rows * D, transcendentals=rows * D
        ),
    )(*ins)


@jax.custom_vjp
def delta_core(queries, keys, values, beta, cumul, segment):
    return delta_core_fwd(queries, keys, values, beta, cumul, segment)[0]


def delta_core_fwd(queries, keys, values, beta, cumul, segment):
    ins = (
        queries,
        keys,
        values,
        beta.T[:, :, None],
        cumul.T[:, :, None],
        cumul.T[:, None, :],
        segment[:, None],
        segment[None, None, :],
    )
    out, inverse, pseudo = delta_call(delta_fwd_kernel, ins, "wwwccrst", "www", 200)
    return out, (ins, inverse, pseudo)


def delta_core_bwd(saved, d_out):
    ins, inverse, pseudo = saved
    d_q, d_k, d_v, d_beta, d_col, d_row = delta_call(
        delta_bwd_kernel, ins + (inverse, pseudo, d_out), "wwwccrstwww", "wwwccr", 120
    )
    d_cumul = (d_col[:, :, 0] - d_row[:, 0, :]).T
    return d_q, d_k, d_v, d_beta[:, :, 0].T, d_cumul, None


delta_core.defvjp(delta_core_fwd, delta_core_bwd)


def delta_rule(queries, key_rows, value_rows, beta_rows, log_decay, segment):
    rows = queries.shape[0]
    cumul = jnp.cumsum(log_decay.reshape(rows // BLOCK, BLOCK, HEADS), axis=1).reshape(rows, HEADS)

    def wide(array):
        return array.reshape(rows, HEADS * HEAD_DIM)

    out = delta_core(
        wide(queries), wide(key_rows), wide(value_rows), beta_rows, cumul, segment
    )
    return out.reshape(rows, HEADS, HEAD_DIM)


def mixer_core(proj, gate_pre, kernel, decay_log, decay_bias, out_gain, segment):
    row_count = proj.shape[0]
    mixed_in = short_conv(proj[:, : 3 * D], kernel, segment)
    heads_shape = (row_count, HEADS, HEAD_DIM)
    query_raw = mixed_in[:, :D].reshape(heads_shape)
    key_raw = mixed_in[:, D : 2 * D].reshape(heads_shape)
    value_rows = mixed_in[:, 2 * D :].reshape(heads_shape)
    queries = (
        query_raw
        * lax.rsqrt(jnp.sum(query_raw * query_raw, axis=-1, keepdims=True) + epsilon)
        * HEAD_DIM ** (-0.5)
    )
    key_rows = key_raw * lax.rsqrt(jnp.sum(key_raw * key_raw, axis=-1, keepdims=True) + epsilon)
    beta_rows = jax.nn.sigmoid(gate_pre[:, HEADS:])
    log_decay = -jnp.exp(decay_log) * jax.nn.softplus(gate_pre[:, :HEADS] + decay_bias)
    delta_out = delta_rule(queries, key_rows, value_rows, beta_rows, log_decay, segment)
    scaled = (
        delta_out
        * lax.rsqrt(jnp.mean(delta_out * delta_out, axis=-1, keepdims=True) + epsilon)
        * out_gain
    )
    gate_part = proj[:, 3 * D :].reshape(heads_shape)
    return (scaled * jax.nn.silu(gate_part)).reshape(row_count, D)


def swiglu(upgate):
    return jax.nn.silu(upgate[:, :FF]) * upgate[:, FF:]


def layer_forward(weights, small_params, block, segment):
    w_in, w_out, w_up, w_down = weights
    gate_weights, norm_gains, kernel, decay_log, decay_bias, out_gain = small_params
    normed_a = rms_scale(block, norm_gains[0]).astype(jnp.bfloat16)
    proj = jnp.dot(normed_a, w_in, preferred_element_type=jnp.float32)
    gate_pre = jnp.dot(normed_a, gate_weights, preferred_element_type=jnp.float32)

    def core_of(proj_in, gate_in, kernel_in, log_in, bias_in, gain_in):
        return mixer_core(proj_in, gate_in, kernel_in, log_in, bias_in, gain_in, segment)

    mixer, core_back = jax.vjp(
        core_of, proj, gate_pre, kernel, decay_log, decay_bias, out_gain
    )
    mixer = mixer.astype(jnp.bfloat16)
    middle = block + jnp.dot(mixer, w_out, preferred_element_type=jnp.float32)
    normed_f = rms_scale(middle, norm_gains[1]).astype(jnp.bfloat16)
    upgate = jnp.dot(normed_f, w_up, preferred_element_type=jnp.float32)
    hidden = swiglu(upgate).astype(jnp.bfloat16)
    result = middle + dot_rows(hidden, w_down)
    return (result, (normed_a, core_back, mixer, middle, normed_f, upgate, hidden))


def core_groups():
    count = lax.axis_size("dp")
    return [list(range(core, count, 2)) for core in range(2)]


def swapped(value):
    return lax.ppermute(value, "dp", [(i, i ^ 1) for i in range(lax.axis_size("dp"))])


def gathered_rows(weight):
    own = lax.all_gather(weight, "dp", axis=0, axis_index_groups=core_groups())
    other = swapped(own)
    even = lax.rem(lax.axis_index("dp"), 2) == 0
    both = jnp.stack([jnp.where(even, own, other), jnp.where(even, other, own)], axis=1)
    return both.reshape(-1, weight.shape[1])


def paired_part(left, right):
    rows, width = left.shape
    count = lax.axis_size("dp")
    halves = left.reshape(rows, count // 2, 2, width // count)
    even = lax.rem(lax.axis_index("dp"), 2) == 0
    first, second = [halves[:, :, i].reshape(rows, width // 2) for i in range(2)]
    theirs = dot_cols(jnp.where(even, second, first), right).astype(jnp.bfloat16)
    mine = dot_cols(jnp.where(even, first, second), right)
    return (mine + swapped(theirs).astype(jnp.float32)).astype(jnp.bfloat16)


def summed_rows(part):
    return lax.psum_scatter(
        part, "dp", scatter_dimension=0, axis_index_groups=core_groups(), tiled=True
    ).astype(jnp.float32)


def layer_backward(weights, small_params, block, saved, grad_out, sums):
    w_in, w_out, w_up, w_down = weights
    gate_weights, norm_gains = small_params[:2]
    normed_a, core_back, mixer, middle, normed_f, upgate, hidden = saved
    g_bf = grad_out.astype(jnp.bfloat16)
    d_hidden = jnp.dot(g_bf, w_down, preferred_element_type=jnp.float32)
    _, swiglu_back = jax.vjp(swiglu, upgate)
    d_upgate = swiglu_back(d_hidden)[0].astype(jnp.bfloat16)
    d_normed_f = dot_rows(d_upgate, w_up)
    _, norm_back_f = jax.vjp(rms_scale, middle, norm_gains[1])
    d_middle, gain_f = norm_back_f(d_normed_f)
    d_middle = d_middle + grad_out
    dm_bf = d_middle.astype(jnp.bfloat16)
    if sums:
        part_up = paired_part(normed_f, d_upgate)
        part_down = paired_part(g_bf, hidden)
        dm_bf, part_up, part_down = lax.optimization_barrier((dm_bf, part_up, part_down))
        sum_up, sum_down = summed_rows(part_up), summed_rows(part_down)
    d_mixer = dot_rows(dm_bf, w_out)
    d_proj, d_gate_pre, d_kernel, d_log, d_bias, d_gain = core_back(d_mixer)
    d_proj = d_proj.astype(jnp.bfloat16)
    d_gate_pre = d_gate_pre.astype(jnp.bfloat16)
    d_normed_a = dot_rows(d_proj, w_in) + dot_rows(d_gate_pre, gate_weights)
    _, norm_back_a = jax.vjp(rms_scale, block, norm_gains[0])
    d_block, gain_a = norm_back_a(d_normed_a)
    d_block = d_block + d_middle
    if not sums:
        return d_block
    big = (
        summed_rows(paired_part(normed_a, d_proj)),
        summed_rows(paired_part(mixer, dm_bf)),
        sum_up,
        sum_down,
    )
    small = (
        dot_cols(normed_a, d_gate_pre),
        jnp.stack([gain_a, gain_f]),
        d_kernel,
        d_log,
        d_bias,
        d_gain,
    )
    return (d_block, big, small)


def summed_small(parts):
    flat = jnp.concatenate([part.reshape(-1) for part in parts])
    count = lax.axis_size("dp")
    if count & (count - 1):
        flat = lax.psum(flat, "dp")
    else:
        step = 1
        while step < count:
            pairs = [(i, i ^ step) for i in range(count)]
            flat = flat + lax.ppermute(flat, "dp", pairs)
            step *= 2
    outs, start = [], 0
    for part in parts:
        outs.append(flat[start : start + part.size].reshape(part.shape))
        start += part.size
    return outs


def local(
    block_input,
    cotangent,
    marks,
    w_in,
    w_out,
    w_up,
    w_down,
    gate_weights,
    norm_gains,
    conv_weights,
    decay_log,
    decay_bias,
    out_gain,
):
    first_section = lax.axis_index("section") == 0
    small_params = (
        gate_weights[0],
        norm_gains[0],
        conv_weights[0],
        decay_log[0],
        decay_bias[0],
        out_gain[0],
    )
    weights = tuple(gathered_rows(weight[0]) for weight in (w_in, w_out, w_up, w_down))
    segment = segment_ids(marks)
    early_out, _ = layer_forward(weights, small_params, block_input, segment)
    arrived = passed_along(early_out.astype(jnp.bfloat16), "section", 1).astype(jnp.float32)
    source = jnp.where(first_section, block_input, arrived)
    layer_out, saved = layer_forward(weights, small_params, source, segment)
    late_grad = layer_backward(weights, small_params, source, saved, cotangent, False)
    returned = passed_along(late_grad.astype(jnp.bfloat16), "section", -1).astype(jnp.float32)
    grad_out = jnp.where(first_section, returned, cotangent)
    input_grad, big, small = layer_backward(weights, small_params, source, saved, grad_out, True)
    return tuple(part[None] for part in (layer_out, input_grad, *big, *summed_small(small)))


def solution(mesh):
    return jax.shard_map(
        local,
        mesh=mesh,
        in_specs=(
            P("dp", None),
            P("dp", None),
            P("dp"),
            P("section", "dp", None),
            P("section", "dp", None),
            P("section", "dp", None),
            P("section", "dp", None),
            P("section", None, None),
            P("section", None, None),
            P("section", None, None),
            P("section", None),
            P("section", None),
            P("section", None),
        ),
        out_specs=(
            P("section", "dp", None),
            P("section", "dp", None),
            P("section", "dp", None),
            P("section", "dp", None),
            P("section", "dp", None),
            P("section", "dp", None),
            P("section", None, None),
            P("section", None, None),
            P("section", None, None),
            P("section", None),
            P("section", None),
            P("section", None),
        ),
        check_vma=False,
    )
```
